32 devices in a mesh: group: 4 (over y, core), slab: 8 (over z, x).
Axes of the slice: x: 2, y: 2, z: 4, core: 2. Of those that a mesh axis runs over, the one named last changes fastest.
Arguments:
- state: float32 [8, 64, 32, 256], P('group', 'slab'), may hold values from -3 to 3
- theta: float32 [8, 32, 16, 128], P('group', 'slab'), may hold values from -2.5 to 2.5
- forcing: float32 [64, 32, 256], P('slab'), may hold values from -6 to 6
- boxes: int32 [6, 4096], replicated, may hold values from 0 to 64, as said below
- observed: float32 [4096], P('slab'), may hold values from -6 to 6
- noise_var: float32 [4096], P('slab'), may hold values from 0.05 to 0.5
- perturb: float32 [8, 4096], P('group', 'slab'), may hold values from -6 to 6
Outputs:
- final_state: float32 [8, 64, 32, 256], P('group', 'slab')
- theta_new: float32 [8, 32, 16, 128], P('group', 'slab')
The draws below stay inside these ranges and needn't reach their ends.
Inputs may be any that keep to these rules, and one draw needn't show every extreme that they name: `boxes`: for every observation z0 < z1 <= 64, y0 < y1 <= 8, x0 < x1 <= 64; a box spans at most 16 planes, 4 tiles along the second dimension and 8 along the third (fewer where the grid is narrower), and these most are reached.
All inputs are finite; a program needn't handle non-finite values.
Results may differ from the reference program's by a relative error of at most 0.00019.
Values sent between devices are 32-bit elements; how exact they have to be, the bound alone decides.
A program may use at most 64 MiB of HBM per device.

```python
import math
import jax
import jax.numpy as jnp
from jax import lax

CZ = 8
NY = 32
NX = 256
MEMBERS = 8
NZ = 64
OBS = 4096


def draw_boxes(key, part):
    keys = jax.random.split(key, 6)
    tiles_y = NY // 4
    tiles_x = NX // 4
    length_z = jax.random.randint(keys[0], (OBS,), 1, 2 * CZ + 1)
    start_z = jax.random.randint(keys[1], (OBS,), 0, NZ - length_z + 1)
    length_y = jax.random.randint(keys[2], (OBS,), 1, min(4, tiles_y) + 1)
    start_y = jax.random.randint(keys[3], (OBS,), 0, tiles_y - length_y + 1)
    length_x = jax.random.randint(keys[4], (OBS,), 1, min(8, tiles_x) + 1)
    start_x = jax.random.randint(keys[5], (OBS,), 0, tiles_x - length_x + 1)
    stacked = jnp.stack([start_z, start_z + length_z, start_y, start_y + length_y, start_x, start_x + length_x])
    return stacked.astype(jnp.int32)


def block_scale(own_key, shape, shards, low, high):
    level, own = 1.0, jax.random.fold_in(own_key, 6)
    for position, parts in shards:
        heights = jnp.exp(jax.random.uniform(jax.random.fold_in(own, position), (parts,), jnp.float32, low / len(shards), high / len(shards)))
        level = level * jnp.repeat(heights, shape[position] // parts).reshape([-1 if axis == position else 1 for axis in range(len(shape))])
    return level


def bell_draw(own_key, extent, spread, reach, shards=(), held_as=jnp.bfloat16):
    loudness = block_scale(own_key, extent, shards, -0.22, 0.18) if shards else 1.0
    array = jax.random.normal(own_key, extent, jnp.float32) * spread * loudness
    return jnp.minimum(jnp.maximum(array, -reach), reach).astype(held_as)


def setup_inputs(seed: int = 0) -> dict:
    streams_of = jax.random.split(jax.random.key(seed), 8)
    state = bell_draw(streams_of[0], (MEMBERS, NZ, NY, NX), 0.5, 3.0, ((0, 4), (1, 8)), jnp.float32)
    theta = bell_draw(streams_of[1], (MEMBERS, NZ // 2, NY // 2, NX // 2), 0.4, 2.5, ((0, 4), (1, 8)), jnp.float32)
    forcing = bell_draw(streams_of[2], (NZ, NY, NX), 1.0, 6.0, ((0, 8),), jnp.float32)
    boxes = draw_boxes(jax.random.fold_in(streams_of[7], 71), 0)
    observed = bell_draw(streams_of[4], (OBS,), 1.0, 6.0, ((0, 8),), jnp.float32)
    noise_var = jnp.clip(jnp.exp(math.log(0.5) - 2.3025851 * jax.random.uniform(streams_of[5], (OBS,), jnp.float32) ** block_scale(streams_of[5], (OBS,), ((0, 8),), -0.2, 0.2)), 0.05, 0.5)
    perturb = bell_draw(streams_of[6], (MEMBERS, OBS), 1.0, 6.0, ((0, 4), (1, 8)), jnp.float32)
    return {"state": state, "theta": theta, "forcing": forcing, "boxes": boxes, "observed": observed, "noise_var": noise_var, "perturb": perturb}


STEP_SIZE = 0.1

def advance(padded, diffusivity, forcing):
    center = padded[:, 1:-1]
    side_pad = jnp.pad(center, ((0, 0), (0, 0), (1, 1), (1, 1)))
    beside_all = padded[:, 2:] + padded[:, :-2]
    beside_all = beside_all + side_pad[:, :, 2:, 1:-1] + side_pad[:, :, :-2, 1:-1]
    beside_all = beside_all + side_pad[:, :, 1:-1, 2:] + side_pad[:, :, 1:-1, :-2]
    change = diffusivity * (beside_all - 6.0 * center) + 0.5 * center * (1.0 - center * center) + forcing
    return center + STEP_SIZE * change

def upsample(params):
    return jnp.repeat(jnp.repeat(jnp.repeat(params, 2, axis=1), 2, axis=2), 2, axis=3)

def reference(state, theta, forcing, boxes, observed, noise_var, perturb):
    diffusivity = 0.5 * jnp.exp(upsample(theta))
    current = state
    for sweep in range(2):
        padded = jnp.pad(current, ((0, 0), (1, 1), (0, 0), (0, 0)))
        current = advance(padded, diffusivity, forcing[None])
    members = current.shape[0]
    tiles = current.reshape(members, NZ, NY // 4, 4, NX // 4, 4).sum(axis=(3, 5))
    table = jnp.cumsum(jnp.cumsum(jnp.cumsum(tiles, axis=1), axis=2), axis=3)
    table = jnp.pad(table, ((0, 0), (1, 0), (1, 0), (1, 0)))
    lower_z, upper_z = (boxes[0], boxes[1])
    lower_y, upper_y = (boxes[2], boxes[3])
    lower_x, upper_x = (boxes[4], boxes[5])
    total = table[:, upper_z, upper_y, upper_x] - table[:, lower_z, upper_y, upper_x]
    total = total - table[:, upper_z, lower_y, upper_x] - table[:, upper_z, upper_y, lower_x]
    total = total + table[:, lower_z, lower_y, upper_x] + table[:, lower_z, upper_y, lower_x]
    total = total + table[:, upper_z, lower_y, lower_x] - table[:, lower_z, lower_y, lower_x]
    count = ((upper_z - lower_z) * (upper_y - lower_y) * (upper_x - lower_x) * 16).astype(jnp.float32)
    predicted = total / count[None]
    scale = jnp.sqrt(jnp.float32(members - 1))
    anomaly = (predicted - lax.optimization_barrier(jnp.mean(predicted, axis=0, keepdims=True))) / scale
    misfit = observed[None] + jnp.sqrt(noise_var)[None] * perturb - predicted
    weighted = anomaly / noise_var[None]
    inner = jnp.dot(weighted, anomaly.T, precision=lax.Precision.HIGHEST)
    cross = jnp.dot(weighted, misfit.T, precision=lax.Precision.HIGHEST)
    identity = jnp.eye(members, dtype=jnp.float32)
    factor = jnp.linalg.cholesky(identity + inner)
    gain = jax.scipy.linalg.cho_solve((factor, True), cross)
    mixing = identity + (gain - lax.optimization_barrier(jnp.mean(gain, axis=0, keepdims=True))) / scale
    flat_theta = theta.reshape(members, -1)
    updated = jnp.dot(mixing.T, flat_theta, precision=lax.Precision.HIGHEST)
    return (current, updated.reshape(theta.shape))
```

```python
import functools
import math

import jax
import jax.numpy as jnp
from jax import lax
from jax.experimental import pallas as pl
from jax.experimental.pallas import tpu as pltpu
from jax.sharding import PartitionSpec as P

STEP_SIZE = 0.1
LANES = 128
TILE = 4
MESH = pl.DeviceIdType.MESH
HIGHEST = lax.Precision.HIGHEST


def remote(src, dst, send, recv, device):
    return pltpu.make_async_remote_copy(
        src_ref=src, dst_ref=dst, send_sem=send, recv_sem=recv, device_id=device, device_id_type=MESH
    )


def drain(ref, sem):
    pltpu.make_async_copy(ref, ref, sem).wait()


def split_dot(left, right):
    return jnp.dot(left, right, precision=HIGHEST, preferred_element_type=jnp.float32)


def kernel(
    groups, slabs, sub,
    state_ref, theta_ref, forcing_ref, boxes_ref, observed_ref, noise_ref, perturb_ref,
    final_ref, theta_new_ref,
    mid, diff, halo, maskx, halves, tile_rows, part_send, part_recv, pert_all, theta_all, sums_send, sums_recv,
    halo_send, halo_recv, theta_send_sem, theta_recv_sem, pert_send_sem, pert_recv_sem,
    part_send_sem, part_recv_sem, sums_send_sem, sums_recv_sem,
):
    mem, planes, rows, cols = state_ref.shape
    coarse_z, coarse_y, coarse_x = theta_ref.shape[1:]
    tiles_y = rows // TILE
    members = groups * mem
    total = groups * slabs
    obs_total = boxes_ref.shape[1]
    obs_slab = obs_total // slabs
    g = lax.axis_index("group")
    s = lax.axis_index("slab")
    me = s * groups + g

    barrier = pltpu.get_barrier_semaphore()

    def greet(step, carry):
        other = lax.rem(me + step, total)
        pl.semaphore_signal(
            barrier, inc=1, device_id=(lax.rem(other, groups), other // groups), device_id_type=MESH
        )
        return carry

    lax.fori_loop(1, total, greet, 0)

    lane = lax.broadcasted_iota(jnp.int32, (rows, cols), 1)
    row = lax.broadcasted_iota(jnp.int32, (rows, cols), 0)

    spread_x = (
        lax.broadcasted_iota(jnp.int32, (coarse_x, cols), 1) // 2
        == lax.broadcasted_iota(jnp.int32, (coarse_x, cols), 0)
    ).astype(jnp.float32)
    spread_y = (
        lax.broadcasted_iota(jnp.int32, (rows, coarse_y), 0) // 2
        == lax.broadcasted_iota(jnp.int32, (rows, coarse_y), 1)
    ).astype(jnp.float32)
    coarse = 0.5 * jnp.exp(theta_ref[...].reshape(mem * coarse_z * coarse_y, coarse_x))
    wide = split_dot(coarse, spread_x)
    for m in range(mem):
        for z in range(coarse_z):
            start = (m * coarse_z + z) * coarse_y
            diff[m, z] = split_dot(spread_y, wide[start : start + coarse_y])

    def step_plane(center, below, above, diffusivity, forcing):
        beside = below + above
        beside = beside + jnp.where(row == rows - 1, 0.0, pltpu.roll(center, rows - 1, 0))
        beside = beside + jnp.where(row == 0, 0.0, pltpu.roll(center, 1, 0))
        beside = beside + jnp.where(lane == cols - 1, 0.0, pltpu.roll(center, cols - 1, 1))
        beside = beside + jnp.where(lane == 0, 0.0, pltpu.roll(center, 1, 1))
        change = (
            diffusivity * (beside - 6.0 * center)
            + 0.5 * center * (1.0 - center * center)
            + forcing
        )
        return center + STEP_SIZE * change

    def inner_planes(src, dst):
        def body(z, carry):
            for m in range(mem):
                dst[m, z] = step_plane(
                    src[m, z], src[m, z - 1], src[m, z + 1], diff[m, z // 2], forcing_ref[z]
                )
            return carry

        lax.fori_loop(1, planes - 1, body, 0)

    def edge_plane(src, dst, sweep, side):
        z = 0 if side == 0 else planes - 1
        for m in range(mem):
            outer = halo[sweep, side, m]
            below = outer if side == 0 else src[m, z - 1]
            above = src[m, z + 1] if side == 0 else outer
            dst[m, z] = step_plane(src[m, z], below, above, diff[m, z // 2], forcing_ref[z])

    inner_planes(state_ref, mid)
    theta_all[g] = theta_ref[...]
    chunk = obs_slab // sub
    own = lax.rem(g, sub)
    own_cols = pl.ds(pl.multiple_of(own * chunk, LANES), chunk)
    pert_all[g] = perturb_ref[:, own_cols]

    pl.semaphore_wait(barrier, total - 1)

    def halo_copy(src, sweep, side):
        plane = 0 if side == 0 else planes - 1
        other = s - 1 if side == 0 else s + 1
        return remote(
            src.at[:, plane],
            halo.at[sweep, 1 - side],
            halo_send.at[sweep, side],
            halo_recv.at[sweep, 1 - side],
            (g, other),
        )

    def has(side):
        return s > 0 if side == 0 else s < slabs - 1

    def start_halo(src, sweep, side):
        @pl.when(has(side))
        def _():
            halo_copy(src, sweep, side).start()

    def wait_halo(sweep, side):
        @pl.when(has(side))
        def _():
            drain(halo.at[sweep, side], halo_recv.at[sweep, side])

        @pl.when(jnp.logical_not(has(side)))
        def _():
            halo[sweep, side] = jnp.zeros_like(halo[sweep, side])

    for side in range(2):
        start_halo(state_ref, 0, side)

    def share(step, carry):
        other = lax.rem(g + step, groups)
        want = lax.rem(other, sub)
        remote(
            perturb_ref.at[:, pl.ds(pl.multiple_of(want * chunk, LANES), chunk)],
            pert_all.at[g], pert_send_sem, pert_recv_sem, (other, s),
        ).start()
        remote(theta_ref, theta_all.at[g], theta_send_sem, theta_recv_sem, (other, s)).start()
        return carry

    lax.fori_loop(1, groups, share, 0)

    width = min(obs_slab, 512)
    tile_x = lax.broadcasted_iota(jnp.int32, (cols, width), 0) // TILE

    def build_mask(block, carry):
        at = pl.ds(pl.multiple_of(block * width, LANES), width)
        low = boxes_ref[4:5, at]
        high = boxes_ref[5:6, at]
        inside = jnp.where((tile_x >= low) & (tile_x < high), 1.0, 0.0)
        maskx[:, at] = inside.astype(jnp.bfloat16)
        return carry

    lax.fori_loop(0, obs_total // width, build_mask, 0)

    for side in range(2):
        wait_halo(0, side)
        edge_plane(state_ref, mid, 0, side)
        start_halo(mid, 1, side)
    inner_planes(mid, final_ref)
    for side in range(2):
        wait_halo(1, side)
        edge_plane(mid, final_ref, 1, side)

    small_lane = lax.broadcasted_iota(jnp.int32, (tiles_y, cols), 1) % TILE

    def collect(z, carry):
        for m in range(mem):
            for h in range(cols // LANES):
                halves[m, z, h] = final_ref[m, z, :, h * LANES : (h + 1) * LANES]
            parts = []
            for h in range(cols // LANES):
                part = halves[m, z, h, pl.ds(0, tiles_y, stride=TILE), :]
                for k in range(1, TILE):
                    part = part + halves[m, z, h, pl.ds(k, tiles_y, stride=TILE), :]
                parts.append(part)
            band = jnp.concatenate(parts, axis=1)
            band = band + pltpu.roll(band, 1, 1)
            band = band + pltpu.roll(band, 2, 1)
            high = band.astype(jnp.bfloat16).astype(jnp.float32)
            rest = band - high
            middle = rest.astype(jnp.bfloat16).astype(jnp.float32)
            low = rest - middle
            packed = jnp.where(
                small_lane == 3,
                high,
                jnp.where(
                    small_lane == 2,
                    pltpu.roll(middle, cols - 1, 1),
                    jnp.where(small_lane == 1, pltpu.roll(low, cols - 2, 1), 0.0),
                ),
            )
            tile_rows[m, z] = packed
        return carry

    lax.fori_loop(0, planes, collect, 0)
    left = tile_rows[...].reshape(mem * planes * tiles_y, cols).astype(jnp.bfloat16)
    tile_y = lax.broadcasted_iota(jnp.int32, (tiles_y, obs_slab), 0)

    def observe(step, carry):
        to = lax.rem(s + 1 + step, slabs)
        at = pl.ds(pl.multiple_of(to * obs_slab, LANES), obs_slab)
        along = jnp.dot(left, maskx[:, at], preferred_element_type=jnp.float32)
        box = boxes_ref[:, at]
        in_y = jnp.where((tile_y >= box[2:3]) & (tile_y < box[3:4]), 1.0, 0.0)
        sums = [jnp.zeros((tiles_y, obs_slab), jnp.float32) for _ in range(mem)]
        for z in range(planes):
            depth = s * planes + z
            in_z = jnp.where((depth >= box[0:1]) & (depth < box[1:2]), 1.0, 0.0)
            for m in range(mem):
                start = (m * planes + z) * tiles_y
                sums[m] = sums[m] + along[start : start + tiles_y] * in_z
        for m in range(mem):
            value = jnp.sum(sums[m] * in_y, axis=0, keepdims=True)
            for c in range(sub):
                part_send[to, c, m : m + 1, :] = value[:, c * chunk : (c + 1) * chunk]
        for k in range(groups):
            @pl.when(to * groups + k != me)
            def _():
                remote(
                    part_send.at[to, k % sub], part_recv.at[me], part_send_sem, part_recv_sem, (k, to)
                ).start()

        return carry

    lax.fori_loop(0, slabs, observe, 0)
    part_recv[me] = part_send[s, own]
    drain(part_recv.at[pl.ds(0, total - 1)], part_recv_sem)
    if groups > 1:
        drain(pert_all.at[pl.ds(0, groups - 1)], pert_recv_sem)

    pieces = []
    for k in range(groups):
        piece = part_recv[k]
        for t in range(1, slabs):
            piece = piece + part_recv[t * groups + k]
        pieces.append(piece)
    sums = jnp.concatenate(pieces, axis=0)
    perturbs = jnp.concatenate([pert_all[k] for k in range(groups)], axis=0)
    at = pl.ds(pl.multiple_of(s * obs_slab + own * chunk, LANES), chunk)
    box = boxes_ref[:, at]
    count = (box[1:2] - box[0:1]) * (box[3:4] - box[2:3]) * (box[5:6] - box[4:5]) * (TILE * TILE)
    predicted = sums / count.astype(jnp.float32)
    noise = noise_ref[:, own_cols]
    scale = math.sqrt(members - 1)
    anomaly = (predicted - jnp.mean(predicted, axis=0, keepdims=True)) / scale
    misfit = observed_ref[:, own_cols] + jnp.sqrt(noise) * perturbs - predicted
    weighted = anomaly / noise
    if sub != groups:
        weighted = weighted * (sub / groups)

    per_row = LANES // members
    packs = 2 * members // per_row
    small = (members, LANES)
    lane_m = lax.broadcasted_iota(jnp.int32, small, 1)
    row_m = lax.broadcasted_iota(jnp.int32, small, 0)
    for r in range(packs):
        packed = jnp.zeros(small, jnp.float32)
        for slot in range(per_row):
            j = r * per_row + slot
            other = anomaly[j : j + 1] if j < members else misfit[j - members : j - members + 1]
            value = jnp.sum(weighted * other, axis=1, keepdims=True)
            packed = packed + jnp.where(lane_m == slot * members + row_m, value, 0.0)
        sums_send[r : r + 1, :] = jnp.sum(packed, axis=0, keepdims=True)
    sums_recv[me] = sums_send[...]

    def spread(step, carry):
        other = lax.rem(me + step, total)
        remote(
            sums_send, sums_recv.at[me], sums_send_sem, sums_recv_sem,
            (lax.rem(other, groups), other // groups),
        ).start()
        return carry

    lax.fori_loop(1, total, spread, 0)
    drain(sums_recv.at[pl.ds(0, total - 1)], sums_recv_sem)
    if total <= 64:
        whole = sums_recv[0]
        for t in range(1, total):
            whole = whole + sums_recv[t]
    else:
        whole = lax.fori_loop(1, total, lambda t, c: c + sums_recv[t], sums_recv[0])

    system = jnp.where(lane_m == row_m, 1.0, 0.0)
    for j in range(2 * members):
        r, slot = j // per_row, j % per_row
        value = jnp.sum(
            jnp.where(lane_m == slot * members + row_m, whole[r : r + 1], 0.0), axis=1, keepdims=True
        )
        system = system + jnp.where(lane_m == j, value, 0.0)
    for k in range(members):
        pivot = system[k : k + 1] / system[k : k + 1, k : k + 1]
        system = jnp.where(row_m == k, pivot, system - system[:, k : k + 1] * pivot)
    mixing = (system - jnp.mean(system, axis=0, keepdims=True)) / scale
    mixing = mixing + jnp.where(lane_m == row_m + members, 1.0, 0.0)
    if groups > 1:
        drain(theta_all.at[pl.ds(0, groups - 1)], theta_recv_sem)
    for m in range(mem):
        column = jnp.sum(
            jnp.where(lane_m == members + g * mem + m, mixing, 0.0), axis=1, keepdims=True
        )
        column = jnp.broadcast_to(column, (members, coarse_x))
        fresh = jnp.zeros(theta_ref.shape[1:], jnp.float32)
        for k in range(members):
            fresh = fresh + theta_all[k // mem, k % mem] * column[k : k + 1][None]
        theta_new_ref[m] = fresh

    for sweep in range(2):
        for side in range(2):
            @pl.when(has(side))
            def _():
                drain(halo.at[sweep, side], halo_send.at[sweep, side])

    if groups > 1:
        drain(pert_all.at[pl.ds(0, groups - 1)], pert_send_sem)
        drain(theta_all.at[pl.ds(0, groups - 1)], theta_send_sem)
    drain(part_recv.at[pl.ds(0, total - 1)], part_send_sem)
    drain(sums_recv.at[pl.ds(0, total - 1)], sums_send_sem)


def local(groups, slabs, state, theta, forcing, boxes, observed, noise_var, perturb):
    mem, planes, rows, cols = state.shape
    total = groups * slabs
    obs_total = boxes.shape[1]
    obs_slab = obs_total // slabs
    sub = min(groups, obs_slab // LANES)
    chunk = obs_slab // sub
    members = groups * mem
    packs = 2 * members * members // LANES
    f32 = jnp.float32
    vmem = pl.BlockSpec(memory_space=pltpu.VMEM)
    dma = pltpu.SemaphoreType.DMA
    return pl.pallas_call(
        functools.partial(kernel, groups, slabs, sub),
        name="window",
        out_shape=(
            jax.ShapeDtypeStruct(state.shape, f32),
            jax.ShapeDtypeStruct(theta.shape, f32),
        ),
        in_specs=[vmem] * 7,
        out_specs=(vmem, vmem),
        scratch_shapes=[
            pltpu.VMEM(state.shape, f32),
            pltpu.VMEM((mem, theta.shape[1], rows, cols), f32),
            pltpu.VMEM((2, 2, mem, rows, cols), f32),
            pltpu.VMEM((cols, obs_total), jnp.bfloat16),
            pltpu.VMEM((mem, planes, cols // LANES, rows, LANES), f32),
            pltpu.VMEM((mem, planes, rows // TILE, cols), f32),
            pltpu.VMEM((slabs, sub, mem, chunk), f32),
            pltpu.VMEM((total, mem, chunk), f32),
            pltpu.VMEM((groups, mem, chunk), f32),
            pltpu.VMEM((groups,) + theta.shape, f32),
            pltpu.VMEM((packs, LANES), f32),
            pltpu.VMEM((total, packs, LANES), f32),
            dma((2, 2)), dma((2, 2)), dma, dma, dma, dma, dma, dma, dma, dma,
        ],
        compiler_params=pltpu.CompilerParams(collective_id=0, has_side_effects=True),
    )(state, theta, forcing, boxes, observed.reshape(1, -1), noise_var.reshape(1, -1), perturb)


def solution(mesh):
    return jax.shard_map(
        functools.partial(local, mesh.shape["group"], mesh.shape["slab"]),
        mesh=mesh,
        in_specs=(
            P("group", "slab", None, None),
            P("group", "slab", None, None),
            P("slab", None, None),
            P(),
            P("slab"),
            P("slab"),
            P("group", "slab"),
        ),
        out_specs=(P("group", "slab", None, None), P("group", "slab", None, None)),
        check_vma=False,
    )
```

```python
import functools
import math

import jax
import jax.numpy as jnp
from jax import lax
from jax.experimental import pallas as pl
from jax.experimental.pallas import tpu as pltpu
from jax.sharding import PartitionSpec as P

STEP_SIZE = 0.1
LANES = 128
TILE = 4
MESH = pl.DeviceIdType.MESH
HIGHEST = lax.Precision.HIGHEST


def remote(src, dst, send, recv, device):
    return pltpu.make_async_remote_copy(
        src_ref=src, dst_ref=dst, send_sem=send, recv_sem=recv, device_id=device, device_id_type=MESH
    )


def drain(ref, sem):
    pltpu.make_async_copy(ref, ref, sem).wait()


def split_dot(left, right):
    return jnp.dot(left, right, precision=HIGHEST, preferred_element_type=jnp.float32)


def kernel(
    groups, slabs, sub,
    state_hbm, theta_hbm, forcing_hbm, boxes_hbm, observed_hbm, noise_hbm, perturb_hbm,
    final_ref, theta_new_ref,
    state_ref, forcing_ref, boxes_ref, observed_ref, noise_ref,
    mid, diff, halo, maskx, halves, tile_rows, part_sum,
    part_send, part_recv, pert_all, theta_all, sums_send, sums_recv,
    load_sem, halo_send, halo_recv, theta_send_sem, theta_recv_sem, pert_send_sem, pert_recv_sem,
    part_send_sem, part_recv_sem, sums_send_sem, sums_recv_sem,
):
    mem, planes, rows, cols = state_ref.shape
    coarse_z, coarse_y, coarse_x = theta_hbm.shape[1:]
    tiles_y = rows // TILE
    members = groups * mem
    total = groups * slabs
    obs_total = boxes_ref.shape[1]
    obs_slab = obs_total // slabs
    chunk = obs_slab // sub
    g = lax.axis_index("group")
    s = lax.axis_index("slab")
    me = s * groups + g
    own = lax.rem(g, sub)
    own_cols = pl.ds(pl.multiple_of(own * chunk, LANES), chunk)

    def wrap(value, size):
        return jnp.where(value >= size, value - size, value)

    def each_slab(body):
        if total <= 64:
            for i in range(slabs):
                half = (i + 1) // 2
                rel = (slabs // 2 + (half if i % 2 == 0 else -half)) % slabs
                body(wrap(s + rel, slabs), rel == 0)
        else:

            def loop(i, carry):
                half = lax.div(i + 1, 2)
                rel = slabs // 2 + jnp.where(lax.rem(i, 2) == 0, half, -half)
                body(lax.rem(s + rel, slabs), None)
                return carry

            lax.fori_loop(0, slabs, loop, 0)

    def each_peer(to, here, send):
        if here is None:
            for k in range(groups):
                @pl.when((to != s) | (g != k))
                def _():
                    send(k)
        elif here:
            for step in range(1, groups):
                send(wrap(g + step, groups))
        else:
            for k in range(groups):
                send(k)

    barrier = pltpu.get_barrier_semaphore()

    def greet(to, here):
        each_peer(
            to, here,
            lambda k: pl.semaphore_signal(barrier, inc=1, device_id=(k, to), device_id_type=MESH),
        )

    each_slab(greet)

    loads = [
        pltpu.make_async_copy(src, dst, load_sem.at[i])
        for i, (src, dst) in enumerate(
            (
                (theta_hbm, theta_all.at[g]),
                (state_hbm, state_ref),
                (forcing_hbm, forcing_ref),
                (boxes_hbm, boxes_ref),
                (perturb_hbm.at[:, own_cols], pert_all.at[g]),
                (observed_hbm, observed_ref),
                (noise_hbm, noise_ref),
            )
        )
    ]
    for load in loads:
        load.start()

    lane = lax.broadcasted_iota(jnp.int32, (rows, cols), 1)
    row = lax.broadcasted_iota(jnp.int32, (rows, cols), 0)

    spread_x = (
        lax.broadcasted_iota(jnp.int32, (coarse_x, cols), 1) // 2
        == lax.broadcasted_iota(jnp.int32, (coarse_x, cols), 0)
    ).astype(jnp.float32)
    spread_y = (
        lax.broadcasted_iota(jnp.int32, (rows, coarse_y), 0) // 2
        == lax.broadcasted_iota(jnp.int32, (rows, coarse_y), 1)
    ).astype(jnp.float32)
    loads[0].wait()
    coarse = 0.5 * jnp.exp(theta_all[g].reshape(mem * coarse_z * coarse_y, coarse_x))
    wide = split_dot(coarse, spread_x)
    for m in range(mem):
        for z in range(coarse_z):
            start = (m * coarse_z + z) * coarse_y
            diff[m, z] = split_dot(spread_y, wide[start : start + coarse_y])

    def step_plane(center, below, above, diffusivity, forcing):
        beside = below + above
        beside = beside + jnp.where(row == rows - 1, 0.0, pltpu.roll(center, rows - 1, 0))
        beside = beside + jnp.where(row == 0, 0.0, pltpu.roll(center, 1, 0))
        beside = beside + jnp.where(lane == cols - 1, 0.0, pltpu.roll(center, cols - 1, 1))
        beside = beside + jnp.where(lane == 0, 0.0, pltpu.roll(center, 1, 1))
        change = (
            diffusivity * (beside - 6.0 * center)
            + 0.5 * center * (1.0 - center * center)
            + forcing
        )
        return center + STEP_SIZE * change

    def inner_planes(src, dst):
        def body(z, carry):
            for m in range(mem):
                dst[m, z] = step_plane(
                    src[m, z], src[m, z - 1], src[m, z + 1], diff[m, z // 2], forcing_ref[z]
                )
            return carry

        lax.fori_loop(1, planes - 1, body, 0)

    def edge_plane(src, dst, sweep, side):
        z = 0 if side == 0 else planes - 1
        for m in range(mem):
            outer = halo[sweep, side, m]
            below = outer if side == 0 else src[m, z - 1]
            above = src[m, z + 1] if side == 0 else outer
            dst[m, z] = step_plane(src[m, z], below, above, diff[m, z // 2], forcing_ref[z])

    loads[1].wait()
    loads[2].wait()
    inner_planes(state_ref, mid)

    pl.semaphore_wait(barrier, total - 1)

    def halo_copy(src, sweep, side):
        plane = 0 if side == 0 else planes - 1
        other = s - 1 if side == 0 else s + 1
        return remote(
            src.at[:, plane],
            halo.at[sweep, 1 - side],
            halo_send.at[sweep, side],
            halo_recv.at[sweep, 1 - side],
            (g, other),
        )

    def has(side):
        return s > 0 if side == 0 else s < slabs - 1

    def start_halo(src, sweep, side):
        @pl.when(has(side))
        def _():
            halo_copy(src, sweep, side).start()

    def wait_halo(sweep, side):
        @pl.when(has(side))
        def _():
            drain(halo.at[sweep, side], halo_recv.at[sweep, side])

        @pl.when(jnp.logical_not(has(side)))
        def _():
            halo[sweep, side] = jnp.zeros_like(halo[sweep, side])

    for side in range(2):
        start_halo(state_hbm, 0, side)

    for step in range(1, groups):
        other = wrap(g + step, groups)
        want = lax.rem(other, sub)
        remote(
            perturb_hbm.at[:, pl.ds(pl.multiple_of(want * chunk, LANES), chunk)],
            pert_all.at[g], pert_send_sem, pert_recv_sem, (other, s),
        ).start()
        remote(theta_hbm, theta_all.at[g], theta_send_sem, theta_recv_sem, (other, s)).start()

    for load in loads[3:]:
        load.wait()
    tile_x = lax.broadcasted_iota(jnp.int32, (cols, obs_slab), 0) // TILE

    def build_mask(block, carry):
        at = pl.ds(pl.multiple_of(block * obs_slab, LANES), obs_slab)
        low = boxes_ref[4:5, at]
        high = boxes_ref[5:6, at]
        inside = jnp.where((tile_x >= low) & (tile_x < high), 1.0, 0.0)
        maskx[:, at] = inside.astype(jnp.bfloat16)
        return carry

    lax.fori_loop(0, slabs, build_mask, 0)

    for side in range(2):
        wait_halo(0, side)
        edge_plane(state_ref, mid, 0, side)
        start_halo(mid, 1, side)
    inner_planes(mid, final_ref)

    small_lane = lax.broadcasted_iota(jnp.int32, (tiles_y, cols), 1) % TILE

    def collect(z):
        for m in range(mem):
            for h in range(cols // LANES):
                halves[m, z, h] = final_ref[m, z, :, h * LANES : (h + 1) * LANES]
            parts = []
            for h in range(cols // LANES):
                part = halves[m, z, h, pl.ds(0, tiles_y, stride=TILE), :]
                for k in range(1, TILE):
                    part = part + halves[m, z, h, pl.ds(k, tiles_y, stride=TILE), :]
                parts.append(part)
            band = jnp.concatenate(parts, axis=1)
            band = band + pltpu.roll(band, 1, 1)
            band = band + pltpu.roll(band, 2, 1)
            high = band.astype(jnp.bfloat16).astype(jnp.float32)
            rest = band - high
            middle = rest.astype(jnp.bfloat16).astype(jnp.float32)
            low = rest - middle
            tile_rows[z, m] = jnp.where(
                small_lane == 3,
                high,
                jnp.where(
                    small_lane == 2,
                    pltpu.roll(middle, cols - 1, 1),
                    jnp.where(small_lane == 1, pltpu.roll(low, cols - 2, 1), 0.0),
                ),
            )

    def weigh(left, at, zs, sums):
        along = jnp.dot(left, maskx[:, at], preferred_element_type=jnp.float32)
        low = boxes_ref[0:1, at]
        high = boxes_ref[1:2, at]
        for i, z in enumerate(zs):
            depth = s * planes + z
            in_z = jnp.where((depth >= low) & (depth < high), 1.0, 0.0)
            for m in range(mem):
                start = (i * mem + m) * tiles_y
                term = along[start : start + tiles_y] * in_z
                sums[m] = term if sums[m] is None else sums[m] + term
        return sums

    def collect_inner(z, carry):
        collect(z)
        return carry

    lax.fori_loop(1, planes - 1, collect_inner, 0)
    inner_rows = tile_rows[1 : planes - 1].reshape((planes - 2) * mem * tiles_y, cols)
    inner_rows = inner_rows.astype(jnp.bfloat16)

    def observe_inner(block, carry):
        at = pl.ds(pl.multiple_of(block * obs_slab, LANES), obs_slab)
        sums = weigh(inner_rows, at, range(1, planes - 1), [None] * mem)
        for m in range(mem):
            part_sum[m, :, at] = sums[m]
        return carry

    lax.fori_loop(0, slabs, observe_inner, 0, unroll=2)

    for side in range(2):
        wait_halo(1, side)
        edge_plane(mid, final_ref, 1, side)
        collect(0 if side == 0 else planes - 1)
    edge_rows = jnp.concatenate(
        [tile_rows[z].reshape(mem * tiles_y, cols) for z in (0, planes - 1)], axis=0
    ).astype(jnp.bfloat16)
    tile_y = lax.broadcasted_iota(jnp.int32, (tiles_y, obs_slab), 0)

    def observe(to, here):
        at = pl.ds(pl.multiple_of(to * obs_slab, LANES), obs_slab)
        sums = weigh(edge_rows, at, (0, planes - 1), [part_sum[m, :, at] for m in range(mem)])
        in_y = jnp.where((tile_y >= boxes_ref[2:3, at]) & (tile_y < boxes_ref[3:4, at]), 1.0, 0.0)
        for m in range(mem):
            value = jnp.sum(sums[m] * in_y, axis=0, keepdims=True)
            for c in range(sub):
                part_send[to, c, m : m + 1, :] = value[:, c * chunk : (c + 1) * chunk]

        def send(k):
            which = k % sub if isinstance(k, int) else lax.rem(k, sub)
            remote(
                part_send.at[to, which], part_recv.at[me], part_send_sem, part_recv_sem, (k, to)
            ).start()

        each_peer(to, here, send)

    each_slab(observe)
    part_recv[me] = part_send[s, own]
    drain(part_recv.at[pl.ds(0, total - 1)], part_recv_sem)
    if groups > 1:
        drain(pert_all.at[pl.ds(0, groups - 1)], pert_recv_sem)

    pieces = []
    for k in range(groups):
        piece = part_recv[k]
        for t in range(1, slabs):
            piece = piece + part_recv[t * groups + k]
        pieces.append(piece)
    sums = jnp.concatenate(pieces, axis=0)
    perturbs = jnp.concatenate([pert_all[k] for k in range(groups)], axis=0)
    at = pl.ds(pl.multiple_of(s * obs_slab + own * chunk, LANES), chunk)
    box = boxes_ref[:, at]
    count = (box[1:2] - box[0:1]) * (box[3:4] - box[2:3]) * (box[5:6] - box[4:5]) * (TILE * TILE)
    predicted = sums / count.astype(jnp.float32)
    noise = noise_ref[:, own_cols]
    scale = math.sqrt(members - 1)
    anomaly = (predicted - jnp.mean(predicted, axis=0, keepdims=True)) / scale
    misfit = observed_ref[:, own_cols] + jnp.sqrt(noise) * perturbs - predicted
    weighted = anomaly / noise
    if sub != groups:
        weighted = weighted * (sub / groups)

    per_row = LANES // members
    packs = 2 * members // per_row
    small = (members, LANES)
    lane_m = lax.broadcasted_iota(jnp.int32, small, 1)
    row_m = lax.broadcasted_iota(jnp.int32, small, 0)
    for r in range(packs):
        packed = jnp.zeros(small, jnp.float32)
        for slot in range(per_row):
            j = r * per_row + slot
            other = anomaly[j : j + 1] if j < members else misfit[j - members : j - members + 1]
            value = jnp.sum(weighted * other, axis=1, keepdims=True)
            packed = packed + jnp.where(lane_m == slot * members + row_m, value, 0.0)
        sums_send[r : r + 1, :] = jnp.sum(packed, axis=0, keepdims=True)
    sums_recv[me] = sums_send[...]

    def spread(to, here):
        each_peer(
            to, here,
            lambda k: remote(
                sums_send, sums_recv.at[me], sums_send_sem, sums_recv_sem, (k, to)
            ).start(),
        )

    each_slab(spread)
    drain(sums_recv.at[pl.ds(0, total - 1)], sums_recv_sem)
    if total <= 64:
        whole = sums_recv[0]
        for t in range(1, total):
            whole = whole + sums_recv[t]
    else:
        whole = lax.fori_loop(1, total, lambda t, c: c + sums_recv[t], sums_recv[0])

    system = jnp.where(lane_m == row_m, 1.0, 0.0)
    for j in range(2 * members):
        r, slot = j // per_row, j % per_row
        value = jnp.sum(
            jnp.where(lane_m == slot * members + row_m, whole[r : r + 1], 0.0), axis=1, keepdims=True
        )
        system = system + jnp.where(lane_m == j, value, 0.0)
    for k in range(members):
        pivot = system[k : k + 1] / system[k : k + 1, k : k + 1]
        system = jnp.where(row_m == k, pivot, system - system[:, k : k + 1] * pivot)
    mixing = (system - jnp.mean(system, axis=0, keepdims=True)) / scale
    mixing = mixing + jnp.where(lane_m == row_m + members, 1.0, 0.0)
    if groups > 1:
        drain(theta_all.at[pl.ds(0, groups - 1)], theta_recv_sem)
    for m in range(mem):
        column = jnp.sum(
            jnp.where(lane_m == members + g * mem + m, mixing, 0.0), axis=1, keepdims=True
        )
        column = jnp.broadcast_to(column, (members, coarse_x))
        fresh = jnp.zeros(theta_new_ref.shape[1:], jnp.float32)
        for k in range(members):
            fresh = fresh + theta_all[k // mem, k % mem] * column[k : k + 1][None]
        theta_new_ref[m] = fresh

    for sweep in range(2):
        for side in range(2):
            @pl.when(has(side))
            def _():
                drain(halo.at[sweep, side], halo_send.at[sweep, side])

    if groups > 1:
        drain(pert_all.at[pl.ds(0, groups - 1)], pert_send_sem)
        drain(theta_all.at[pl.ds(0, groups - 1)], theta_send_sem)
    drain(part_recv.at[pl.ds(0, total - 1)], part_send_sem)
    drain(sums_recv.at[pl.ds(0, total - 1)], sums_send_sem)


def local(groups, slabs, state, theta, forcing, boxes, observed, noise_var, perturb):
    mem, planes, rows, cols = state.shape
    total = groups * slabs
    obs_total = boxes.shape[1]
    obs_slab = obs_total // slabs
    sub = min(groups, obs_slab // LANES)
    chunk = obs_slab // sub
    members = groups * mem
    packs = 2 * members * members // LANES
    f32 = jnp.float32
    vmem = pl.BlockSpec(memory_space=pltpu.VMEM)
    dma = pltpu.SemaphoreType.DMA
    return pl.pallas_call(
        functools.partial(kernel, groups, slabs, sub),
        name="window",
        out_shape=(
            pltpu.VMEM(state.shape, f32),
            pltpu.VMEM(theta.shape, f32),
        ),
        in_specs=[pl.BlockSpec(memory_space=pl.ANY)] * 7,
        out_specs=(vmem, vmem),
        scratch_shapes=[
            pltpu.VMEM(state.shape, f32),
            pltpu.VMEM(forcing.shape, f32),
            pltpu.VMEM(boxes.shape, boxes.dtype),
            pltpu.VMEM((1, obs_slab), f32),
            pltpu.VMEM((1, obs_slab), f32),
            pltpu.VMEM(state.shape, f32),
            pltpu.VMEM((mem, theta.shape[1], rows, cols), f32),
            pltpu.VMEM((2, 2, mem, rows, cols), f32),
            pltpu.VMEM((cols, obs_total), jnp.bfloat16),
            pltpu.VMEM((mem, planes, cols // LANES, rows, LANES), f32),
            pltpu.VMEM((planes, mem, rows // TILE, cols), f32),
            pltpu.VMEM((mem, rows // TILE, obs_total), f32),
            pltpu.VMEM((slabs, sub, mem, chunk), f32),
            pltpu.VMEM((total, mem, chunk), f32),
            pltpu.VMEM((groups, mem, chunk), f32),
            pltpu.VMEM((groups,) + theta.shape, f32),
            pltpu.VMEM((packs, LANES), f32),
            pltpu.VMEM((total, packs, LANES), f32),
            dma((7,)), dma((2, 2)), dma((2, 2)), dma, dma, dma, dma, dma, dma, dma, dma,
        ],
        compiler_params=pltpu.CompilerParams(collective_id=0, has_side_effects=True),
    )(state, theta, forcing, boxes, observed.reshape(1, -1), noise_var.reshape(1, -1), perturb)


def solution(mesh):
    return jax.shard_map(
        functools.partial(local, mesh.shape["group"], mesh.shape["slab"]),
        mesh=mesh,
        in_specs=(
            P("group", "slab", None, None),
            P("group", "slab", None, None),
            P("slab", None, None),
            P(),
            P("slab"),
            P("slab"),
            P("group", "slab"),
        ),
        out_specs=(P("group", "slab", None, None), P("group", "slab", None, None)),
        check_vma=False,
    )
```

```python
import functools
import math

import jax
import jax.numpy as jnp
from jax import lax
from jax.experimental import pallas as pl
from jax.experimental.pallas import tpu as pltpu
from jax.sharding import PartitionSpec as P

STEP_SIZE = 0.1
LANES = 128
TILE = 4
MESH = pl.DeviceIdType.MESH
HIGHEST = lax.Precision.HIGHEST


def remote(src, dst, send, recv, device):
    return pltpu.make_async_remote_copy(
        src_ref=src, dst_ref=dst, send_sem=send, recv_sem=recv, device_id=device, device_id_type=MESH
    )


def drain(ref, sem):
    pltpu.make_async_copy(ref, ref, sem).wait()


def split_dot(left, right):
    return jnp.dot(left, right, precision=HIGHEST, preferred_element_type=jnp.float32)


def kernel(
    groups, slabs, sub,
    state_hbm, theta_hbm, forcing_hbm, boxes_hbm, observed_hbm, noise_hbm, perturb_hbm,
    final_ref, theta_new_ref,
    state_ref, forcing_ref, boxes_ref, observed_ref, noise_ref,
    mid, diff, halo, maskx, halves, tile_rows, part_sum,
    part_send, part_recv, pert_all, theta_all, sums_send, sums_recv,
    load_sem, halo_send, halo_recv, theta_send_sem, theta_recv_sem, pert_send_sem, pert_recv_sem,
    part_send_sem, part_recv_sem, sums_send_sem, sums_recv_sem,
):
    mem, planes, rows, cols = state_ref.shape
    coarse_z, coarse_y, coarse_x = theta_hbm.shape[1:]
    tiles_y = rows // TILE
    members = groups * mem
    total = groups * slabs
    obs_total = boxes_ref.shape[1]
    obs_slab = obs_total // slabs
    chunk = obs_slab // sub
    g = lax.axis_index("group")
    s = lax.axis_index("slab")
    me = s * groups + g
    own = lax.rem(g, sub)
    own_cols = pl.ds(pl.multiple_of(own * chunk, LANES), chunk)

    def wrap(value, size):
        return jnp.where(value >= size, value - size, value)

    def each_slab(body):
        if total <= 64:
            for i in range(slabs):
                half = (i + 1) // 2
                rel = (slabs // 2 + (half if i % 2 == 0 else -half)) % slabs
                body(wrap(s + rel, slabs), rel == 0)
        else:

            def loop(i, carry):
                half = lax.div(i + 1, 2)
                rel = slabs // 2 + jnp.where(lax.rem(i, 2) == 0, half, -half)
                body(lax.rem(s + rel, slabs), None)
                return carry

            lax.fori_loop(0, slabs, loop, 0)

    def each_peer(to, here, send):
        if here is None:
            for k in range(groups):
                @pl.when((to != s) | (g != k))
                def _():
                    send(k)
        elif here:
            for step in range(1, groups):
                send(wrap(g + step, groups))
        else:
            for k in range(groups):
                send(k)

    barrier = pltpu.get_barrier_semaphore()

    def greet(to, here):
        each_peer(
            to, here,
            lambda k: pl.semaphore_signal(barrier, inc=1, device_id=(k, to), device_id_type=MESH),
        )

    each_slab(greet)

    loads = [
        pltpu.make_async_copy(src, dst, load_sem.at[i])
        for i, (src, dst) in enumerate(
            (
                (theta_hbm, theta_all.at[g]),
                (state_hbm, state_ref),
                (forcing_hbm, forcing_ref),
                (boxes_hbm, boxes_ref),
                (perturb_hbm.at[:, own_cols], pert_all.at[g]),
                (observed_hbm, observed_ref),
                (noise_hbm, noise_ref),
            )
        )
    ]
    for load in loads:
        load.start()

    lane = lax.broadcasted_iota(jnp.int32, (rows, cols), 1)
    row = lax.broadcasted_iota(jnp.int32, (rows, cols), 0)

    spread_x = (
        lax.broadcasted_iota(jnp.int32, (coarse_x, cols), 1) // 2
        == lax.broadcasted_iota(jnp.int32, (coarse_x, cols), 0)
    ).astype(jnp.float32)
    spread_y = (
        lax.broadcasted_iota(jnp.int32, (rows, coarse_y), 0) // 2
        == lax.broadcasted_iota(jnp.int32, (rows, coarse_y), 1)
    ).astype(jnp.float32)
    loads[0].wait()
    coarse = 0.5 * jnp.exp(theta_all[g].reshape(mem * coarse_z * coarse_y, coarse_x))
    wide = split_dot(coarse, spread_x)
    for m in range(mem):
        for z in range(coarse_z):
            start = (m * coarse_z + z) * coarse_y
            diff[m, z] = split_dot(spread_y, wide[start : start + coarse_y])

    def step_plane(center, below, above, diffusivity, forcing):
        beside = below + above
        beside = beside + jnp.where(row == rows - 1, 0.0, pltpu.roll(center, rows - 1, 0))
        beside = beside + jnp.where(row == 0, 0.0, pltpu.roll(center, 1, 0))
        beside = beside + jnp.where(lane == cols - 1, 0.0, pltpu.roll(center, cols - 1, 1))
        beside = beside + jnp.where(lane == 0, 0.0, pltpu.roll(center, 1, 1))
        change = (
            diffusivity * (beside - 6.0 * center)
            + 0.5 * center * (1.0 - center * center)
            + forcing
        )
        return center + STEP_SIZE * change

    def inner_planes(src, dst):
        def body(z, carry):
            for m in range(mem):
                dst[m, z] = step_plane(
                    src[m, z], src[m, z - 1], src[m, z + 1], diff[m, z // 2], forcing_ref[z]
                )
            return carry

        lax.fori_loop(1, planes - 1, body, 0)

    def edge_plane(src, dst, sweep, side):
        z = 0 if side == 0 else planes - 1
        for m in range(mem):
            outer = halo[sweep, side, m]
            below = outer if side == 0 else src[m, z - 1]
            above = src[m, z + 1] if side == 0 else outer
            dst[m, z] = step_plane(src[m, z], below, above, diff[m, z // 2], forcing_ref[z])

    loads[1].wait()
    loads[2].wait()
    inner_planes(state_ref, mid)

    pl.semaphore_wait(barrier, total - 1)

    def halo_copy(src, sweep, side):
        plane = 0 if side == 0 else planes - 1
        other = s - 1 if side == 0 else s + 1
        return remote(
            src.at[:, plane],
            halo.at[sweep, 1 - side],
            halo_send.at[sweep, side],
            halo_recv.at[sweep, 1 - side],
            (g, other),
        )

    def has(side):
        return s > 0 if side == 0 else s < slabs - 1

    def start_halo(src, sweep, side):
        @pl.when(has(side))
        def _():
            halo_copy(src, sweep, side).start()

    def wait_halo(sweep, side):
        @pl.when(has(side))
        def _():
            drain(halo.at[sweep, side], halo_recv.at[sweep, side])

        @pl.when(jnp.logical_not(has(side)))
        def _():
            halo[sweep, side] = jnp.zeros_like(halo[sweep, side])

    for side in range(2):
        start_halo(state_hbm, 0, side)

    for step in range(1, groups):
        other = wrap(g + step, groups)
        want = lax.rem(other, sub)
        remote(
            perturb_hbm.at[:, pl.ds(pl.multiple_of(want * chunk, LANES), chunk)],
            pert_all.at[g], pert_send_sem, pert_recv_sem, (other, s),
        ).start()

    for load in loads[3:]:
        load.wait()
    tile_x = lax.broadcasted_iota(jnp.int32, (cols, obs_slab), 0) // TILE

    def build_mask(block, carry):
        at = pl.ds(pl.multiple_of(block * obs_slab, LANES), obs_slab)
        low = boxes_ref[4:5, at]
        high = boxes_ref[5:6, at]
        inside = jnp.where((tile_x >= low) & (tile_x < high), 1.0, 0.0)
        maskx[:, at] = inside.astype(jnp.bfloat16)
        return carry

    lax.fori_loop(0, slabs, build_mask, 0)

    for side in range(2):
        wait_halo(0, side)
        edge_plane(state_ref, mid, 0, side)
        start_halo(mid, 1, side)
    inner_planes(mid, final_ref)

    small_lane = lax.broadcasted_iota(jnp.int32, (tiles_y, cols), 1) % TILE

    def collect(z):
        for m in range(mem):
            for h in range(cols // LANES):
                halves[m, z, h] = final_ref[m, z, :, h * LANES : (h + 1) * LANES]
            parts = []
            for h in range(cols // LANES):
                part = halves[m, z, h, pl.ds(0, tiles_y, stride=TILE), :]
                for k in range(1, TILE):
                    part = part + halves[m, z, h, pl.ds(k, tiles_y, stride=TILE), :]
                parts.append(part)
            band = jnp.concatenate(parts, axis=1)
            band = band + pltpu.roll(band, 1, 1)
            band = band + pltpu.roll(band, 2, 1)
            high = band.astype(jnp.bfloat16).astype(jnp.float32)
            rest = band - high
            middle = rest.astype(jnp.bfloat16).astype(jnp.float32)
            low = rest - middle
            tile_rows[z, m] = jnp.where(
                small_lane == 3,
                high,
                jnp.where(
                    small_lane == 2,
                    pltpu.roll(middle, cols - 1, 1),
                    jnp.where(small_lane == 1, pltpu.roll(low, cols - 2, 1), 0.0),
                ),
            )

    def weigh(left, at, zs, sums):
        along = jnp.dot(left, maskx[:, at], preferred_element_type=jnp.float32)
        low = boxes_ref[0:1, at]
        high = boxes_ref[1:2, at]
        for i, z in enumerate(zs):
            depth = s * planes + z
            in_z = jnp.where((depth >= low) & (depth < high), 1.0, 0.0)
            for m in range(mem):
                start = (i * mem + m) * tiles_y
                term = along[start : start + tiles_y] * in_z
                sums[m] = term if sums[m] is None else sums[m] + term
        return sums

    def collect_inner(z, carry):
        collect(z)
        return carry

    lax.fori_loop(1, planes - 1, collect_inner, 0)
    inner_rows = tile_rows[1 : planes - 1].reshape((planes - 2) * mem * tiles_y, cols)
    inner_rows = inner_rows.astype(jnp.bfloat16)

    def observe_inner(block, carry):
        at = pl.ds(pl.multiple_of(block * obs_slab, LANES), obs_slab)
        sums = weigh(inner_rows, at, range(1, planes - 1), [None] * mem)
        for m in range(mem):
            part_sum[m, :, at] = sums[m]
        return carry

    lax.fori_loop(0, slabs, observe_inner, 0, unroll=2)

    for side in range(2):
        wait_halo(1, side)
        edge_plane(mid, final_ref, 1, side)
        collect(0 if side == 0 else planes - 1)
    edge_rows = jnp.concatenate(
        [tile_rows[z].reshape(mem * tiles_y, cols) for z in (0, planes - 1)], axis=0
    ).astype(jnp.bfloat16)
    tile_y = lax.broadcasted_iota(jnp.int32, (tiles_y, obs_slab), 0)

    def observe(to, here):
        at = pl.ds(pl.multiple_of(to * obs_slab, LANES), obs_slab)
        sums = weigh(edge_rows, at, (0, planes - 1), [part_sum[m, :, at] for m in range(mem)])
        in_y = jnp.where((tile_y >= boxes_ref[2:3, at]) & (tile_y < boxes_ref[3:4, at]), 1.0, 0.0)
        for m in range(mem):
            value = jnp.sum(sums[m] * in_y, axis=0, keepdims=True)
            for c in range(sub):
                part_send[to, c, m : m + 1, :] = value[:, c * chunk : (c + 1) * chunk]

        def send(k):
            which = k % sub if isinstance(k, int) else lax.rem(k, sub)
            remote(
                part_send.at[to, which], part_recv.at[me], part_send_sem, part_recv_sem, (k, to)
            ).start()

        each_peer(to, here, send)

    each_slab(observe)
    for step in range(1, groups):
        other = wrap(g + step, groups)
        remote(theta_hbm, theta_all.at[g], theta_send_sem, theta_recv_sem, (other, s)).start()

    part_recv[me] = part_send[s, own]
    drain(part_recv.at[pl.ds(0, total - 1)], part_recv_sem)
    if groups > 1:
        drain(pert_all.at[pl.ds(0, groups - 1)], pert_recv_sem)

    pieces = []
    for k in range(groups):
        piece = part_recv[k]
        for t in range(1, slabs):
            piece = piece + part_recv[t * groups + k]
        pieces.append(piece)
    sums = jnp.concatenate(pieces, axis=0)
    perturbs = jnp.concatenate([pert_all[k] for k in range(groups)], axis=0)
    at = pl.ds(pl.multiple_of(s * obs_slab + own * chunk, LANES), chunk)
    box = boxes_ref[:, at]
    count = (box[1:2] - box[0:1]) * (box[3:4] - box[2:3]) * (box[5:6] - box[4:5]) * (TILE * TILE)
    predicted = sums / count.astype(jnp.float32)
    noise = noise_ref[:, own_cols]
    scale = math.sqrt(members - 1)
    anomaly = (predicted - jnp.mean(predicted, axis=0, keepdims=True)) / scale
    misfit = observed_ref[:, own_cols] + jnp.sqrt(noise) * perturbs - predicted
    weighted = anomaly / noise

    per_row = LANES // members
    packs = 2 * members // per_row
    small = (members, LANES)
    lane_m = lax.broadcasted_iota(jnp.int32, small, 1)
    row_m = lax.broadcasted_iota(jnp.int32, small, 0)
    for r in range(packs):
        packed = jnp.zeros(small, jnp.float32)
        for slot in range(per_row):
            j = r * per_row + slot
            other = anomaly[j : j + 1] if j < members else misfit[j - members : j - members + 1]
            value = jnp.sum(weighted * other, axis=1, keepdims=True)
            packed = packed + jnp.where(lane_m == slot * members + row_m, value, 0.0)
        sums_send[r : r + 1, :] = jnp.sum(packed, axis=0, keepdims=True)
    sums_recv[s] = sums_send[...]

    def spread(to, here):
        def send():
            remote(
                sums_send, sums_recv.at[s], sums_send_sem, sums_recv_sem, (g, to)
            ).start()

        if here is None:
            pl.when(to != s)(send)
        elif not here:
            send()

    each_slab(spread)
    drain(sums_recv.at[pl.ds(0, slabs - 1)], sums_recv_sem)
    whole = sums_recv[0]
    for t in range(1, slabs):
        whole = whole + sums_recv[t]

    system = jnp.where(lane_m == row_m, 1.0, 0.0)
    for j in range(2 * members):
        r, slot = j // per_row, j % per_row
        value = jnp.sum(
            jnp.where(lane_m == slot * members + row_m, whole[r : r + 1], 0.0), axis=1, keepdims=True
        )
        system = system + jnp.where(lane_m == j, value, 0.0)
    for k in range(members):
        pivot = system[k : k + 1] / system[k : k + 1, k : k + 1]
        system = jnp.where(row_m == k, pivot, system - system[:, k : k + 1] * pivot)
    mixing = (system - jnp.mean(system, axis=0, keepdims=True)) / scale
    mixing = mixing + jnp.where(lane_m == row_m + members, 1.0, 0.0)
    if groups > 1:
        drain(theta_all.at[pl.ds(0, groups - 1)], theta_recv_sem)
    for m in range(mem):
        column = jnp.sum(
            jnp.where(lane_m == members + g * mem + m, mixing, 0.0), axis=1, keepdims=True
        )
        column = jnp.broadcast_to(column, (members, coarse_x))
        fresh = jnp.zeros(theta_new_ref.shape[1:], jnp.float32)
        for k in range(members):
            fresh = fresh + theta_all[k // mem, k % mem] * column[k : k + 1][None]
        theta_new_ref[m] = fresh

    for sweep in range(2):
        for side in range(2):
            @pl.when(has(side))
            def _():
                drain(halo.at[sweep, side], halo_send.at[sweep, side])

    if groups > 1:
        drain(pert_all.at[pl.ds(0, groups - 1)], pert_send_sem)
        drain(theta_all.at[pl.ds(0, groups - 1)], theta_send_sem)
    drain(part_recv.at[pl.ds(0, total - 1)], part_send_sem)
    drain(sums_recv.at[pl.ds(0, slabs - 1)], sums_send_sem)


def local(groups, slabs, state, theta, forcing, boxes, observed, noise_var, perturb):
    mem, planes, rows, cols = state.shape
    total = groups * slabs
    obs_total = boxes.shape[1]
    obs_slab = obs_total // slabs
    sub = 1
    chunk = obs_slab // sub
    members = groups * mem
    packs = 2 * members * members // LANES
    f32 = jnp.float32
    vmem = pl.BlockSpec(memory_space=pltpu.VMEM)
    dma = pltpu.SemaphoreType.DMA
    return pl.pallas_call(
        functools.partial(kernel, groups, slabs, sub),
        name="window",
        out_shape=(
            pltpu.VMEM(state.shape, f32),
            pltpu.VMEM(theta.shape, f32),
        ),
        in_specs=[pl.BlockSpec(memory_space=pl.ANY)] * 7,
        out_specs=(vmem, vmem),
        scratch_shapes=[
            pltpu.VMEM(state.shape, f32),
            pltpu.VMEM(forcing.shape, f32),
            pltpu.VMEM(boxes.shape, boxes.dtype),
            pltpu.VMEM((1, obs_slab), f32),
            pltpu.VMEM((1, obs_slab), f32),
            pltpu.VMEM(state.shape, f32),
            pltpu.VMEM((mem, theta.shape[1], rows, cols), f32),
            pltpu.VMEM((2, 2, mem, rows, cols), f32),
            pltpu.VMEM((cols, obs_total), jnp.bfloat16),
            pltpu.VMEM((mem, planes, cols // LANES, rows, LANES), f32),
            pltpu.VMEM((planes, mem, rows // TILE, cols), f32),
            pltpu.VMEM((mem, rows // TILE, obs_total), f32),
            pltpu.VMEM((slabs, sub, mem, chunk), f32),
            pltpu.VMEM((total, mem, chunk), f32),
            pltpu.VMEM((groups, mem, chunk), f32),
            pltpu.VMEM((groups,) + theta.shape, f32),
            pltpu.VMEM((packs, LANES), f32),
            pltpu.VMEM((slabs, packs, LANES), f32),
            dma((7,)), dma((2, 2)), dma((2, 2)), dma, dma, dma, dma, dma, dma, dma, dma,
        ],
        compiler_params=pltpu.CompilerParams(collective_id=0, has_side_effects=True),
    )(state, theta, forcing, boxes, observed.reshape(1, -1), noise_var.reshape(1, -1), perturb)


def solution(mesh):
    return jax.shard_map(
        functools.partial(local, mesh.shape["group"], mesh.shape["slab"]),
        mesh=mesh,
        in_specs=(
            P("group", "slab", None, None),
            P("group", "slab", None, None),
            P("slab", None, None),
            P(),
            P("slab"),
            P("slab"),
            P("group", "slab"),
        ),
        out_specs=(P("group", "slab", None, None), P("group", "slab", None, None)),
        check_vma=False,
    )
```

```python
import functools
import math

import jax
import jax.numpy as jnp
from jax import lax
from jax.experimental import pallas as pl
from jax.experimental.pallas import tpu as pltpu
from jax.sharding import PartitionSpec as P

STEP_SIZE = 0.1
LANES = 128
TILE = 4
MESH = pl.DeviceIdType.MESH
HIGHEST = lax.Precision.HIGHEST


def remote(src, dst, send, recv, device):
    return pltpu.make_async_remote_copy(
        src_ref=src, dst_ref=dst, send_sem=send, recv_sem=recv, device_id=device, device_id_type=MESH
    )


def drain(ref, sem):
    pltpu.make_async_copy(ref, ref, sem).wait()


def split_dot(left, right):
    return jnp.dot(left, right, precision=HIGHEST, preferred_element_type=jnp.float32)


def kernel(
    groups, slabs, sub,
    state_hbm, theta_hbm, forcing_hbm, boxes_hbm, observed_hbm, noise_hbm, perturb_hbm,
    final_ref, theta_new_ref,
    state_ref, forcing_ref, boxes_ref, observed_ref, noise_ref,
    mid, diff, halo, maskx, halves, tile_rows, part_sum,
    part_send, part_recv, pert_all, theta_all, sums_send, sums_recv,
    load_sem, halo_send, halo_recv, theta_send_sem, theta_recv_sem, pert_send_sem, pert_recv_sem,
    part_send_sem, part_recv_sem, sums_send_sem, sums_recv_sem,
):
    mem, planes, rows, cols = state_ref.shape
    coarse_z, coarse_y, coarse_x = theta_hbm.shape[1:]
    tiles_y = rows // TILE
    members = groups * mem
    total = groups * slabs
    obs_total = boxes_ref.shape[1]
    obs_slab = obs_total // slabs
    chunk = obs_slab // sub
    g = lax.axis_index("group")
    s = lax.axis_index("slab")
    me = s * groups + g
    own = lax.rem(g, sub)
    own_cols = pl.ds(pl.multiple_of(own * chunk, LANES), chunk)

    def wrap(value, size):
        return jnp.where(value >= size, value - size, value)

    def each_slab(body):
        if total <= 64:
            for i in range(slabs):
                half = (i + 1) // 2
                rel = (slabs // 2 + (half if i % 2 == 0 else -half)) % slabs
                body(wrap(s + rel, slabs), rel == 0)
        else:

            def loop(i, carry):
                half = lax.div(i + 1, 2)
                rel = slabs // 2 + jnp.where(lax.rem(i, 2) == 0, half, -half)
                body(lax.rem(s + rel, slabs), None)
                return carry

            lax.fori_loop(0, slabs, loop, 0)

    def each_peer(to, here, send):
        if here is None:
            for k in range(groups):
                @pl.when((to != s) | (g != k))
                def _():
                    send(k)
        elif here:
            for step in range(1, groups):
                send(wrap(g + step, groups))
        else:
            for k in range(groups):
                send(k)

    barrier = pltpu.get_barrier_semaphore()

    def greet(to, here):
        each_peer(
            to, here,
            lambda k: pl.semaphore_signal(barrier, inc=1, device_id=(k, to), device_id_type=MESH),
        )

    each_slab(greet)

    loads = [
        pltpu.make_async_copy(src, dst, load_sem.at[i])
        for i, (src, dst) in enumerate(
            (
                (theta_hbm, theta_all.at[g]),
                (state_hbm, state_ref),
                (forcing_hbm, forcing_ref),
                (boxes_hbm, boxes_ref),
                (perturb_hbm.at[:, own_cols], pert_all.at[g]),
                (observed_hbm, observed_ref),
                (noise_hbm, noise_ref),
            )
        )
    ]
    for load in loads:
        load.start()

    lane = lax.broadcasted_iota(jnp.int32, (rows, cols), 1)
    row = lax.broadcasted_iota(jnp.int32, (rows, cols), 0)

    spread_x = (
        lax.broadcasted_iota(jnp.int32, (coarse_x, cols), 1) // 2
        == lax.broadcasted_iota(jnp.int32, (coarse_x, cols), 0)
    ).astype(jnp.float32)
    spread_y = (
        lax.broadcasted_iota(jnp.int32, (rows, coarse_y), 0) // 2
        == lax.broadcasted_iota(jnp.int32, (rows, coarse_y), 1)
    ).astype(jnp.float32)
    loads[0].wait()
    coarse = 0.5 * jnp.exp(theta_all[g].reshape(mem * coarse_z * coarse_y, coarse_x))
    wide = split_dot(coarse, spread_x)
    for m in range(mem):
        for z in range(coarse_z):
            start = (m * coarse_z + z) * coarse_y
            diff[m, z] = split_dot(spread_y, wide[start : start + coarse_y])

    def step_plane(center, below, above, diffusivity, forcing):
        beside = below + above
        beside = beside + jnp.where(row == rows - 1, 0.0, pltpu.roll(center, rows - 1, 0))
        beside = beside + jnp.where(row == 0, 0.0, pltpu.roll(center, 1, 0))
        beside = beside + jnp.where(lane == cols - 1, 0.0, pltpu.roll(center, cols - 1, 1))
        beside = beside + jnp.where(lane == 0, 0.0, pltpu.roll(center, 1, 1))
        change = (
            diffusivity * (beside - 6.0 * center)
            + 0.5 * center * (1.0 - center * center)
            + forcing
        )
        return center + STEP_SIZE * change

    def inner_planes(src, dst):
        def body(z, carry):
            for m in range(mem):
                dst[m, z] = step_plane(
                    src[m, z], src[m, z - 1], src[m, z + 1], diff[m, z // 2], forcing_ref[z]
                )
            return carry

        lax.fori_loop(1, planes - 1, body, 0)

    def edge_plane(src, dst, sweep, side):
        z = 0 if side == 0 else planes - 1
        for m in range(mem):
            outer = halo[sweep, side, m]
            below = outer if side == 0 else src[m, z - 1]
            above = src[m, z + 1] if side == 0 else outer
            dst[m, z] = step_plane(src[m, z], below, above, diff[m, z // 2], forcing_ref[z])

    loads[1].wait()
    loads[2].wait()
    inner_planes(state_ref, mid)

    pl.semaphore_wait(barrier, total - 1)

    def halo_copy(src, sweep, side):
        plane = 0 if side == 0 else planes - 1
        other = s - 1 if side == 0 else s + 1
        return remote(
            src.at[:, plane],
            halo.at[sweep, 1 - side],
            halo_send.at[sweep, side],
            halo_recv.at[sweep, 1 - side],
            (g, other),
        )

    def has(side):
        return s > 0 if side == 0 else s < slabs - 1

    def start_halo(src, sweep, side):
        @pl.when(has(side))
        def _():
            halo_copy(src, sweep, side).start()

    def wait_halo(sweep, side):
        @pl.when(has(side))
        def _():
            drain(halo.at[sweep, side], halo_recv.at[sweep, side])

        @pl.when(jnp.logical_not(has(side)))
        def _():
            halo[sweep, side] = jnp.zeros_like(halo[sweep, side])

    for side in range(2):
        start_halo(state_hbm, 0, side)

    for step in range(1, groups):
        other = wrap(g + step, groups)
        want = lax.rem(other, sub)
        remote(
            perturb_hbm.at[:, pl.ds(pl.multiple_of(want * chunk, LANES), chunk)],
            pert_all.at[g], pert_send_sem, pert_recv_sem, (other, s),
        ).start()

    for load in loads[3:]:
        load.wait()
    tile_x = lax.broadcasted_iota(jnp.int32, (cols, obs_slab), 0) // TILE

    def build_mask(block, carry):
        at = pl.ds(pl.multiple_of(block * obs_slab, LANES), obs_slab)
        low = boxes_ref[4:5, at]
        high = boxes_ref[5:6, at]
        inside = jnp.where((tile_x >= low) & (tile_x < high), 1.0, 0.0)
        maskx[:, at] = inside.astype(jnp.bfloat16)
        return carry

    lax.fori_loop(0, slabs, build_mask, 0)

    for side in range(2):
        wait_halo(0, side)
        edge_plane(state_ref, mid, 0, side)
        start_halo(mid, 1, side)
    inner_planes(mid, final_ref)

    small_lane = lax.broadcasted_iota(jnp.int32, (tiles_y, cols), 1) % TILE

    def collect(z):
        for m in range(mem):
            for h in range(cols // LANES):
                halves[m, z, h] = final_ref[m, z, :, h * LANES : (h + 1) * LANES]
            parts = []
            for h in range(cols // LANES):
                part = halves[m, z, h, pl.ds(0, tiles_y, stride=TILE), :]
                for k in range(1, TILE):
                    part = part + halves[m, z, h, pl.ds(k, tiles_y, stride=TILE), :]
                parts.append(part)
            band = jnp.concatenate(parts, axis=1)
            band = band + pltpu.roll(band, 1, 1)
            band = band + pltpu.roll(band, 2, 1)
            high = band.astype(jnp.bfloat16).astype(jnp.float32)
            rest = band - high
            middle = rest.astype(jnp.bfloat16).astype(jnp.float32)
            low = rest - middle
            tile_rows[z, m] = jnp.where(
                small_lane == 3,
                high,
                jnp.where(
                    small_lane == 2,
                    pltpu.roll(middle, cols - 1, 1),
                    jnp.where(small_lane == 1, pltpu.roll(low, cols - 2, 1), 0.0),
                ),
            )

    def weigh(left, at, zs, sums):
        along = jnp.dot(left, maskx[:, at], preferred_element_type=jnp.float32)
        low = boxes_ref[0:1, at]
        high = boxes_ref[1:2, at]
        for i, z in enumerate(zs):
            depth = s * planes + z
            in_z = jnp.where((depth >= low) & (depth < high), 1.0, 0.0)
            for m in range(mem):
                start = (i * mem + m) * tiles_y
                term = along[start : start + tiles_y] * in_z
                sums[m] = term if sums[m] is None else sums[m] + term
        return sums

    def collect_inner(z, carry):
        collect(z)
        return carry

    lax.fori_loop(1, planes - 1, collect_inner, 0)
    inner_rows = tile_rows[1 : planes - 1].reshape((planes - 2) * mem * tiles_y, cols)
    inner_rows = inner_rows.astype(jnp.bfloat16)

    def observe_inner(block, carry):
        at = pl.ds(pl.multiple_of(block * obs_slab, LANES), obs_slab)
        sums = weigh(inner_rows, at, range(1, planes - 1), [None] * mem)
        for m in range(mem):
            part_sum[m, :, at] = sums[m]
        return carry

    lax.fori_loop(0, slabs, observe_inner, 0, unroll=2)

    for side in range(2):
        wait_halo(1, side)
        edge_plane(mid, final_ref, 1, side)
        collect(0 if side == 0 else planes - 1)
    edge_rows = jnp.concatenate(
        [tile_rows[z].reshape(mem * tiles_y, cols) for z in (0, planes - 1)], axis=0
    ).astype(jnp.bfloat16)
    tile_y = lax.broadcasted_iota(jnp.int32, (tiles_y, obs_slab), 0)

    def observe(to, here):
        at = pl.ds(pl.multiple_of(to * obs_slab, LANES), obs_slab)
        sums = weigh(edge_rows, at, (0, planes - 1), [part_sum[m, :, at] for m in range(mem)])
        in_y = jnp.where((tile_y >= boxes_ref[2:3, at]) & (tile_y < boxes_ref[3:4, at]), 1.0, 0.0)
        for m in range(mem):
            value = jnp.sum(sums[m] * in_y, axis=0, keepdims=True)
            for c in range(sub):
                part_send[to, c, m : m + 1, :] = value[:, c * chunk : (c + 1) * chunk]

        def send(k):
            which = k % sub if isinstance(k, int) else lax.rem(k, sub)
            remote(
                part_send.at[to, which], part_recv.at[me], part_send_sem, part_recv_sem, (k, to)
            ).start()

        each_peer(to, here, send)

    each_slab(observe)
    for step in range(1, groups):
        other = wrap(g + step, groups)
        remote(theta_hbm, theta_all.at[g], theta_send_sem, theta_recv_sem, (other, s)).start()

    part_recv[me] = part_send[s, own]
    drain(part_recv.at[pl.ds(0, total - 1)], part_recv_sem)
    if groups > 1:
        drain(pert_all.at[pl.ds(0, groups - 1)], pert_recv_sem)

    pieces = []
    for k in range(groups):
        piece = part_recv[k]
        for t in range(1, slabs):
            piece = piece + part_recv[t * groups + k]
        pieces.append(piece)
    sums = jnp.concatenate(pieces, axis=0)
    perturbs = jnp.concatenate([pert_all[k] for k in range(groups)], axis=0)
    at = pl.ds(pl.multiple_of(s * obs_slab + own * chunk, LANES), chunk)
    box = boxes_ref[:, at]
    count = (box[1:2] - box[0:1]) * (box[3:4] - box[2:3]) * (box[5:6] - box[4:5]) * (TILE * TILE)
    predicted = sums / count.astype(jnp.float32)
    noise = noise_ref[:, own_cols]
    scale = math.sqrt(members - 1)
    anomaly = (predicted - jnp.mean(predicted, axis=0, keepdims=True)) / scale
    misfit = observed_ref[:, own_cols] + jnp.sqrt(noise) * perturbs - predicted
    weighted = anomaly / noise

    small = (members, LANES)
    lane_m = lax.broadcasted_iota(jnp.int32, small, 1)
    row_m = lax.broadcasted_iota(jnp.int32, small, 0)
    placed = jnp.zeros(small, jnp.float32)
    for j in range(2 * members):
        other = anomaly[j : j + 1] if j < members else misfit[j - members : j - members + 1]
        value = jnp.sum(weighted * other, axis=1, keepdims=True)
        placed = placed + jnp.where(lane_m == j, value, 0.0)
    sums_send[...] = placed
    sums_recv[s] = sums_send[...]

    def spread(to, here):
        def send():
            remote(
                sums_send, sums_recv.at[s], sums_send_sem, sums_recv_sem, (g, to)
            ).start()

        if here is None:
            pl.when(to != s)(send)
        elif not here:
            send()

    each_slab(spread)
    drain(sums_recv.at[pl.ds(0, slabs - 1)], sums_recv_sem)
    whole = sums_recv[0]
    for t in range(1, slabs):
        whole = whole + sums_recv[t]

    system = whole + jnp.where(lane_m == row_m, 1.0, 0.0)
    for k in range(members):
        pivot = system[k : k + 1] / system[k : k + 1, k : k + 1]
        system = jnp.where(row_m == k, pivot, system - system[:, k : k + 1] * pivot)
    mixing = (system - jnp.mean(system, axis=0, keepdims=True)) / scale
    mixing = mixing + jnp.where(lane_m == row_m + members, 1.0, 0.0)
    if groups > 1:
        drain(theta_all.at[pl.ds(0, groups - 1)], theta_recv_sem)
    for m in range(mem):
        column = jnp.sum(
            jnp.where(lane_m == members + g * mem + m, mixing, 0.0), axis=1, keepdims=True
        )
        column = jnp.broadcast_to(column, (members, coarse_x))
        fresh = jnp.zeros(theta_new_ref.shape[1:], jnp.float32)
        for k in range(members):
            fresh = fresh + theta_all[k // mem, k % mem] * column[k : k + 1][None]
        theta_new_ref[m] = fresh

    for sweep in range(2):
        for side in range(2):
            @pl.when(has(side))
            def _():
                drain(halo.at[sweep, side], halo_send.at[sweep, side])

    if groups > 1:
        drain(pert_all.at[pl.ds(0, groups - 1)], pert_send_sem)
        drain(theta_all.at[pl.ds(0, groups - 1)], theta_send_sem)
    drain(part_recv.at[pl.ds(0, total - 1)], part_send_sem)
    drain(sums_recv.at[pl.ds(0, slabs - 1)], sums_send_sem)


def local(groups, slabs, state, theta, forcing, boxes, observed, noise_var, perturb):
    mem, planes, rows, cols = state.shape
    total = groups * slabs
    obs_total = boxes.shape[1]
    obs_slab = obs_total // slabs
    sub = 1
    chunk = obs_slab // sub
    members = groups * mem
    f32 = jnp.float32
    vmem = pl.BlockSpec(memory_space=pltpu.VMEM)
    dma = pltpu.SemaphoreType.DMA
    return pl.pallas_call(
        functools.partial(kernel, groups, slabs, sub),
        name="window",
        out_shape=(
            pltpu.VMEM(state.shape, f32),
            pltpu.VMEM(theta.shape, f32),
        ),
        in_specs=[pl.BlockSpec(memory_space=pl.ANY)] * 7,
        out_specs=(vmem, vmem),
        scratch_shapes=[
            pltpu.VMEM(state.shape, f32),
            pltpu.VMEM(forcing.shape, f32),
            pltpu.VMEM(boxes.shape, boxes.dtype),
            pltpu.VMEM((1, obs_slab), f32),
            pltpu.VMEM((1, obs_slab), f32),
            pltpu.VMEM(state.shape, f32),
            pltpu.VMEM((mem, theta.shape[1], rows, cols), f32),
            pltpu.VMEM((2, 2, mem, rows, cols), f32),
            pltpu.VMEM((cols, obs_total), jnp.bfloat16),
            pltpu.VMEM((mem, planes, cols // LANES, rows, LANES), f32),
            pltpu.VMEM((planes, mem, rows // TILE, cols), f32),
            pltpu.VMEM((mem, rows // TILE, obs_total), f32),
            pltpu.VMEM((slabs, sub, mem, chunk), f32),
            pltpu.VMEM((total, mem, chunk), f32),
            pltpu.VMEM((groups, mem, chunk), f32),
            pltpu.VMEM((groups,) + theta.shape, f32),
            pltpu.VMEM((members, LANES), f32),
            pltpu.VMEM((slabs, members, LANES), f32),
            dma((7,)), dma((2, 2)), dma((2, 2)), dma, dma, dma, dma, dma, dma, dma, dma,
        ],
        compiler_params=pltpu.CompilerParams(collective_id=0, has_side_effects=True),
    )(state, theta, forcing, boxes, observed.reshape(1, -1), noise_var.reshape(1, -1), perturb)


def solution(mesh):
    return jax.shard_map(
        functools.partial(local, mesh.shape["group"], mesh.shape["slab"]),
        mesh=mesh,
        in_specs=(
            P("group", "slab", None, None),
            P("group", "slab", None, None),
            P("slab", None, None),
            P(),
            P("slab"),
            P("slab"),
            P("group", "slab"),
        ),
        out_specs=(P("group", "slab", None, None), P("group", "slab", None, None)),
        check_vma=False,
    )
```
